32 devices in a mesh: rows: 8 (over y, x, core), rhs: 4 (over z).
Axes of the slice: x: 2, y: 2, z: 4, core: 2. Of those that a mesh axis runs over, the one named last changes fastest.
Arguments:
- samples: float32 [65536, 16], P(('rows', 'rhs')), may hold values from -5 to 5
- freq_table: float32 [4096, 16], replicated, may hold values from -3 to 3
- feature_seeds: int32 [512], replicated, may hold values from 0 to 4095
- phases: float32 [512], replicated, may hold values from -3.140625 to 3.140625
- treatment_features: bfloat16 [65536, 512], P('rows', 'rhs'), may hold values from -2.5 to 2.5, as said below
Outputs:
- coefficients: float32 [512, 512], replicated
- fitted: float32 [65536, 512], P(('rows', 'rhs'))
The draws below stay inside these ranges and needn't reach their ends.
Inputs may be any that keep to these rules, and one draw needn't show every extreme that they name: `treatment_features`: treatment features depend on the instrument values.
All inputs are finite; a program needn't handle non-finite values.
Results may differ from the reference program's by a relative error of at most 0.0008.
The reference program's roundings to bfloat16 on the way count: a program that leaves them out, or rounds other values in their place, can miss the bound.
Values may be sent and summed in bfloat16 or wider, within the bound.
A program may use at most 64 MiB of HBM per device.

```python
import jax
import jax.numpy as jnp
from jax import lax

M = 512
P_SIZE = 512
DX = 16
NFREQ = 4096
TOTAL = 65536


def joint_values(key):
    base = jax.random.fold_in(key, 7)
    values = jnp.clip(jax.random.normal(jax.random.fold_in(base, 1), (TOTAL, DX), jnp.float32), -5.0, 5.0)
    mixing = jax.random.normal(jax.random.fold_in(base, 2), (DX, P_SIZE), jnp.float32) * 0.4
    noise = jax.random.normal(jax.random.fold_in(base, 3), (TOTAL, P_SIZE), jnp.float32)
    targets = jnp.clip(jnp.tanh(jnp.dot(values, mixing)) + 0.3 * noise, -2.5, 2.5)
    return (values, targets)


def draw_samples(key, part):
    return joint_values(key)[0]


def draw_treatment_features(key, part):
    return joint_values(key)[1].astype(jnp.bfloat16)


def plant(array, stream_key, least, top_value):
    longest = array.shape.index(max(array.shape))
    spots = []
    for shift in (0, 1):
        where = [jax.random.randint(jax.random.fold_in(stream_key, axis), (), 0, length) for axis, length in enumerate(array.shape)]
        where[longest] = (where[longest] + shift) % array.shape[longest]
        spots.append(tuple(where))
    return array.at[spots[0]].set(least).at[spots[1]].set(top_value)


def gaussian(rng, extent, deviation, reach, kind=jnp.bfloat16):
    entries = deviation * jax.random.normal(rng, extent, jnp.float32)
    return jnp.clip(entries, min=-reach, max=reach).astype(kind)


def setup_inputs(seed: int = 0) -> dict:
    streams_of = jax.random.split(jax.random.key(seed), 6)
    return {
        "samples": draw_samples(jax.random.fold_in(streams_of[5], 71), 0),
        "freq_table": gaussian(streams_of[1], (NFREQ, DX), 0.5, 3.0, jnp.float32),
        "feature_seeds": plant(jax.random.randint(streams_of[2], (M,), 0, NFREQ), jax.random.fold_in(streams_of[2], 1), 0, NFREQ - 1).astype(jnp.int32),
        "phases": jnp.clip(jax.random.uniform(streams_of[3], (M,), jnp.float32, -3.140625, 3.140625), -3.140625, 3.140625),
        "treatment_features": draw_treatment_features(jax.random.fold_in(streams_of[5], 71), 0),
    }


ridge = 0.05

def solve_with(factor, right):
    lower = lax.linalg.triangular_solve(factor, right, left_side=True, lower=True)
    return lax.linalg.triangular_solve(factor, lower, left_side=True, lower=True, transpose_a=True)

def reference(samples, freq_table, feature_seeds, phases, treatment_features):
    count = samples.shape[0]
    freqs = freq_table[feature_seeds.astype(jnp.int32)]
    angles = jnp.dot(samples.astype(jnp.float32), freqs.T.astype(jnp.float32), precision=lax.Precision.HIGHEST, preferred_element_type=jnp.float32) + phases
    instruments = (jnp.sqrt(jnp.float32(2.0)) * jnp.cos(angles)).astype(jnp.bfloat16)
    gram = jnp.dot(instruments.T.astype(jnp.float32), instruments.astype(jnp.float32), preferred_element_type=jnp.float32) / count
    gram = gram + ridge * jnp.eye(gram.shape[0], dtype=jnp.float32)
    cross = jnp.dot(instruments.T.astype(jnp.float32), treatment_features.astype(jnp.float32), preferred_element_type=jnp.float32) / count
    factor = jnp.linalg.cholesky(gram)
    coefficients = solve_with(factor, cross)
    fitted = jnp.dot(instruments.astype(jnp.float32), coefficients.astype(jnp.bfloat16).astype(jnp.float32), preferred_element_type=jnp.float32)
    return (coefficients, fitted)
```

```python
import functools
import math

import jax
import jax.numpy as jnp
from jax import lax
from jax.experimental import pallas as pl
from jax.experimental.pallas import tpu as pltpu
from jax.sharding import PartitionSpec as P

ridge = 0.05
MESH = pl.DeviceIdType.MESH
HIGHEST = lax.Precision.HIGHEST
VMEM = pl.BlockSpec(memory_space=pltpu.VMEM)
NT = (((1,), (1,)), ((), ()))
TILE = 128
SIN_TERMS = [
    (-1.0) ** k * math.pi ** (2 * k + 1) / math.factorial(2 * k + 1) for k in range(7)
]


def split_low(x):
    high = lax.reduce_precision(x, 8, 7)
    rest = x - high
    middle = lax.reduce_precision(rest, 8, 7)
    low = rest - middle
    return tuple(t.astype(jnp.bfloat16) for t in (high, middle, low))


def gather_kernel(group, x_ref, out_ref, send, recv):
    me = lax.axis_index("rhs")
    barrier = pltpu.get_barrier_semaphore()
    for d in range(1, group):
        pl.semaphore_signal(
            barrier, inc=1, device_id={"rhs": lax.rem(me + d, group)}, device_id_type=MESH
        )
    pl.semaphore_wait(barrier, group - 1)
    copies = []
    for d in range(1, group):
        copy = pltpu.make_async_remote_copy(
            src_ref=x_ref,
            dst_ref=out_ref.at[me],
            send_sem=send.at[d],
            recv_sem=recv.at[d],
            device_id={"rhs": lax.rem(me + d, group)},
            device_id_type=MESH,
        )
        copy.start()
        copies.append(copy)
    out_ref[me] = x_ref[...]
    for copy in copies:
        copy.wait()


def gather_samples(x):
    group = lax.axis_size("rhs")
    return pl.pallas_call(
        functools.partial(gather_kernel, group),
        out_shape=jax.ShapeDtypeStruct((group,) + x.shape, x.dtype),
        in_specs=[VMEM],
        out_specs=VMEM,
        scratch_shapes=[pltpu.SemaphoreType.DMA((group,))] * 2,
        compiler_params=pltpu.CompilerParams(collective_id=0, has_side_effects=True),
    )(x)


def panel_kernel(me_ref, x_ref, f_ref, t_ref, acc_ref, own_ref, phi_ref):
    block, part = pl.program_id(0), pl.program_id(1)
    me = me_ref[0]
    panel = t_ref.shape[1]
    chunk = t_ref.shape[0]
    x = x_ref[0]
    high = x.astype(jnp.bfloat16)
    rest = x - high.astype(jnp.float32)
    middle = rest.astype(jnp.bfloat16)
    low = (rest - middle.astype(jnp.float32)).astype(jnp.bfloat16)
    ones = jnp.ones(x.shape, jnp.bfloat16)
    rows = jnp.concatenate([high, high, middle, middle, high, low, ones], axis=0)
    turns = jnp.dot(f_ref[...], rows, preferred_element_type=jnp.float32)
    r = turns - jnp.round(turns)
    u = r * r
    scale = math.sqrt(2.0 * math.sqrt(2.0))
    s = jnp.full_like(u, SIN_TERMS[-1] * scale)
    for term in reversed(SIN_TERMS[:-1]):
        s = s * u + term * scale
    s = s * r
    phi = (math.sqrt(2.0) - s * s).astype(jnp.bfloat16)
    phi_ref[...] = phi

    @pl.when(jnp.logical_and(block == 0, part == 0))
    def _():
        acc_ref[...] = jnp.zeros_like(acc_ref)

    mine = phi_ref[pl.ds(pl.multiple_of(me * panel, panel), panel), :]
    acc_ref[:, :panel] += lax.dot_general(
        phi, mine, NT, preferred_element_type=jnp.float32
    )
    acc_ref[:, panel:] += jnp.dot(phi, t_ref[...], preferred_element_type=jnp.float32)

    @pl.when(block == me)
    def _():
        own_ref[part] = phi


def panels(me, gathered, freqs, targets):
    group, depth, own = gathered.shape
    features = freqs.shape[0]
    panel = targets.shape[1]
    chunk = min(own, 1024)
    parts = own // chunk
    return pl.pallas_call(
        panel_kernel,
        grid_spec=pltpu.PrefetchScalarGridSpec(
            num_scalar_prefetch=1,
            grid=(group, parts),
            in_specs=[
                pl.BlockSpec((1, depth, chunk), lambda i, j, me: (i, 0, j)),
                pl.BlockSpec(freqs.shape, lambda i, j, me: (0, 0)),
                pl.BlockSpec((chunk, panel), lambda i, j, me: (i * parts + j, 0)),
            ],
            out_specs=[
                pl.BlockSpec((features, 2 * panel), lambda i, j, me: (0, 0)),
                pl.BlockSpec((parts, features, chunk), lambda i, j, me: (0, 0, 0)),
            ],
            scratch_shapes=[pltpu.VMEM((features, chunk), jnp.bfloat16)],
        ),
        out_shape=[
            jax.ShapeDtypeStruct((features, 2 * panel), jnp.float32),
            jax.ShapeDtypeStruct((parts, features, chunk), jnp.bfloat16),
        ],
    )(me, gathered, freqs, targets)


def reduce_kernel(R, Z, w_ref, out_ref, got, send, recv, zsend, zrecv, psend, precv, csend, crecv):
    r, z = lax.axis_index("rows"), lax.axis_index("rhs")
    core = lax.rem(r, 2)
    sibling = r + 1 - 2 * core
    barrier = pltpu.get_barrier_semaphore()
    for d in range(1, R):
        pl.semaphore_signal(
            barrier, inc=1, device_id={"rows": lax.rem(r + d, R)}, device_id_type=MESH
        )
    for d in range(1, Z):
        pl.semaphore_signal(
            barrier, inc=1, device_id={"rhs": lax.rem(z + d, Z)}, device_id_type=MESH
        )
    pl.semaphore_wait(barrier, R + Z - 2)

    copies = []
    for d in range(1, R):
        peer = lax.rem(r + d, R)
        copy = pltpu.make_async_remote_copy(
            src_ref=w_ref.at[peer],
            dst_ref=got.at[d],
            send_sem=send.at[d],
            recv_sem=recv.at[d],
            device_id={"rows": peer},
            device_id_type=MESH,
        )
        copy.start()
        copies.append(copy)
    total = w_ref[r]
    for d, copy in enumerate(copies, 1):
        copy.wait()
        total = total + got[d]
    out_ref[r, z] = total

    copies = []
    for d in range(1, Z):
        copy = pltpu.make_async_remote_copy(
            src_ref=out_ref.at[r, z],
            dst_ref=out_ref.at[r, z],
            send_sem=zsend.at[d],
            recv_sem=zrecv.at[d],
            device_id={"rhs": lax.rem(z + d, Z)},
            device_id_type=MESH,
        )
        copy.start()
        copies.append(copy)
    for copy in copies:
        copy.wait()

    half = R // 2
    spot = r // 2

    def to_sibling(i, where):
        copy = pltpu.make_async_remote_copy(
            src_ref=out_ref.at[where],
            dst_ref=out_ref.at[where],
            send_sem=csend.at[i],
            recv_sem=crecv.at[i],
            device_id={"rows": sibling},
            device_id_type=MESH,
        )
        copy.start()
        return copy

    across = []
    for d in range(1, half):
        copy = pltpu.make_async_remote_copy(
            src_ref=out_ref.at[r],
            dst_ref=out_ref.at[r],
            send_sem=psend.at[d],
            recv_sem=precv.at[d],
            device_id={"rows": lax.rem(spot + d, half) * 2 + core},
            device_id_type=MESH,
        )
        copy.start()
        across.append(copy)
    local = [to_sibling(0, r)]
    for d, copy in enumerate(across, 1):
        copy.wait()
        local.append(to_sibling(d, lax.rem(spot - d + half, half) * 2 + core))
    for copy in local:
        copy.wait()


def reduce_panels(w):
    R, Z = lax.axis_size("rows"), lax.axis_size("rhs")
    features, width = w.shape
    rows = features // R
    sems = pltpu.SemaphoreType.DMA
    return pl.pallas_call(
        functools.partial(reduce_kernel, R, Z),
        out_shape=jax.ShapeDtypeStruct((R, Z, rows, width), jnp.float32),
        in_specs=[VMEM],
        out_specs=VMEM,
        scratch_shapes=[pltpu.VMEM((R, rows, width), jnp.float32)]
        + [sems((R,))] * 2
        + [sems((Z,))] * 2
        + [sems((R,))] * 4,
        compiler_params=pltpu.CompilerParams(collective_id=1, has_side_effects=True),
    )(w.reshape(R, rows, width))


def invert_two(a, b, d):
    scale = 1.0 / (a * d - b * b)
    return d * scale, -b * scale, a * scale


def invert_four(p):
    e0, e1, e2 = invert_two(p[0][0], p[0][1], p[1][1])
    y00 = e0 * p[0][2] + e1 * p[1][2]
    y01 = e0 * p[0][3] + e1 * p[1][3]
    y10 = e1 * p[0][2] + e2 * p[1][2]
    y11 = e1 * p[0][3] + e2 * p[1][3]
    s0 = p[2][2] - (p[0][2] * y00 + p[1][2] * y10)
    s1 = p[2][3] - (p[0][2] * y01 + p[1][2] * y11)
    s2 = p[3][3] - (p[0][3] * y01 + p[1][3] * y11)
    t0, t1, t2 = invert_two(s0, s1, s2)
    q02 = -(y00 * t0 + y01 * t1)
    q03 = -(y00 * t1 + y01 * t2)
    q12 = -(y10 * t0 + y11 * t1)
    q13 = -(y10 * t1 + y11 * t2)
    q00 = e0 - (q02 * y00 + q03 * y01)
    q01 = e1 - (q02 * y10 + q03 * y11)
    q11 = e2 - (q12 * y10 + q13 * y11)
    return [
        [q00, q01, q02, q03],
        [q01, q11, q12, q13],
        [q02, q12, t0, t1],
        [q03, q13, t1, t2],
    ]


def invert_block(ref, dst):
    q = 4
    groups = TILE // 8
    a = [ref[8 * i : 8 * i + 8, :] for i in range(groups)]
    lane = lax.broadcasted_iota(jnp.int32, (8, TILE), 1)
    sub = lax.broadcasted_iota(jnp.int32, (8, TILE), 0)
    lane1 = lane[:1]
    for k in range(0, TILE, q):
        g, o = k // 8, k % 8
        c = [
            [jnp.broadcast_to(v[:, k + j : k + j + 1], (8, TILE)) for j in range(q)]
            for v in a
        ]
        p = [[c[g][j][o + i : o + i + 1, :] for j in range(q)] for i in range(q)]
        inv = invert_four(p)
        inside = jnp.logical_and(lane >= k, lane < k + q)
        pivot = [
            jnp.where(lane1 == k + i, 1.0, jnp.where(inside[:1], 0.0, a[g][o + i : o + i + 1, :]))
            for i in range(q)
        ]
        w = [sum(inv[i][j] * pivot[j] for j in range(q)) for i in range(q)]
        wb = [jnp.broadcast_to(v, (8, TILE)) for v in w]
        new = []
        for i in range(groups):
            v = jnp.where(inside, 0.0, a[i])
            v = v - ((c[i][0] * wb[0] + c[i][1] * wb[1]) + (c[i][2] * wb[2] + c[i][3] * wb[3]))
            if i == g:
                for j in range(q):
                    v = jnp.where(sub == o + j, wb[j], v)
            new.append(v)
        a = new
    for i in range(groups):
        dst[8 * i : 8 * i + 8, :] = a[i]


def solve_kernel(count, big_ref, coef_ref, low_ref, gram, right, inverse):
    R, Z, rows, width = big_ref.shape
    panel = width // 2
    size = gram.shape[0]
    for r in range(R):
        for z in range(Z):
            here = (slice(r * rows, (r + 1) * rows), slice(z * panel, (z + 1) * panel))
            gram[here] = big_ref[r, z, :, :panel] * (1.0 / count)
            right[here] = big_ref[r, z, :, panel:] * (1.0 / count)
    row = lax.broadcasted_iota(jnp.int32, (TILE, TILE), 0)
    col = lax.broadcasted_iota(jnp.int32, (TILE, TILE), 1)
    eye = jnp.where(row == col, jnp.float32(ridge), 0.0)
    blocks = size // TILE
    dot = functools.partial(jnp.dot, precision=HIGHEST, preferred_element_type=jnp.float32)

    def at(i):
        return slice(i * TILE, (i + 1) * TILE)

    for k in range(blocks):
        gram[at(k), at(k)] += eye
    tail = lambda k: slice((k + 1) * TILE, size)

    @pl.loop(0, blocks)
    def _(k):
        begin = pl.multiple_of(k * TILE, TILE)
        mine = pl.ds(begin, TILE)
        inverse[1] = gram[mine, mine]
        invert_block(inverse.at[1], inverse.at[0])
        inv = inverse[0]
        right[mine, :] = dot(inv, right[mine, :])
        gram_row = dot(inv, gram[mine, :])

        @pl.loop(k + 1, blocks)
        def _(i):
            below = pl.ds(pl.multiple_of(i * TILE, TILE), TILE)
            left = gram[below, mine]
            gram[below, :] -= dot(left, gram_row)
            right[below, :] -= dot(left, right[mine, :])

        gram[mine, :] = gram_row

    for k in reversed(range(blocks)):
        value = right[at(k), :]
        if k + 1 < blocks:
            value = value - dot(gram[at(k), tail(k)], right[tail(k), :])
            right[at(k), :] = value
        coef_ref[at(k), :] = value
        low_ref[at(k), :] = value.astype(jnp.bfloat16)


def solve(count, big):
    R, Z, rows, width = big.shape
    size, columns = R * rows, Z * width // 2
    return pl.pallas_call(
        functools.partial(solve_kernel, count),
        out_shape=[
            jax.ShapeDtypeStruct((size, columns), jnp.float32),
            jax.ShapeDtypeStruct((size, columns), jnp.bfloat16),
        ],
        in_specs=[VMEM],
        out_specs=[VMEM, VMEM],
        scratch_shapes=[
            pltpu.VMEM((size, size), jnp.float32),
            pltpu.VMEM((size, columns), jnp.float32),
            pltpu.VMEM((2, TILE, TILE), jnp.float32),
        ],
    )(big)


def body(samples, freq_table, feature_seeds, phases, treatment_features):
    count = samples.shape[0] * lax.axis_size("rows") * lax.axis_size("rhs")
    turn = jnp.float32(1.0 / (2.0 * math.pi))
    high, middle, low = split_low(freq_table[feature_seeds] * turn)
    shift = jnp.stack(split_low(phases * turn), axis=1)
    shift = jnp.pad(shift, ((0, 0), (0, high.shape[1] - shift.shape[1])))
    freqs = jnp.concatenate([high, middle, high, middle, low, high, shift], axis=1)
    gathered = gather_samples(samples.T)
    me = lax.axis_index("rhs").astype(jnp.int32).reshape(1)
    w, own = panels(me, gathered, freqs, treatment_features)
    coefficients, low_coef = solve(count, reduce_panels(w))
    fitted = lax.dot_general(
        own, low_coef, (((1,), (0,)), ((), ())), preferred_element_type=jnp.float32
    ).reshape(samples.shape[0], low_coef.shape[1])
    return (coefficients, fitted)


def solution(mesh):
    placed = (P(("rows", "rhs"), None), P(), P(), P(), P("rows", "rhs"))
    return jax.shard_map(
        body, mesh=mesh, in_specs=placed, out_specs=(P(), P(("rows", "rhs"), None)), check_vma=False
    )
```

```python
import functools
import math

import jax
import jax.numpy as jnp
from jax import lax
from jax.experimental import pallas as pl
from jax.experimental.pallas import tpu as pltpu
from jax.sharding import PartitionSpec as P

ridge = 0.05
MESH = pl.DeviceIdType.MESH
HIGHEST = lax.Precision.HIGHEST
VMEM = pl.BlockSpec(memory_space=pltpu.VMEM)
NT = (((1,), (1,)), ((), ()))
TILE = 128
SIN_TERMS = [3.1415926532437486, -5.167712741221454, 2.5501627947182053, -0.5992474048759052, 0.08203123002136099, -0.00700050017770637]


def split_low(x):
    high = lax.reduce_precision(x, 8, 7)
    rest = x - high
    middle = lax.reduce_precision(rest, 8, 7)
    low = rest - middle
    return tuple(t.astype(jnp.bfloat16) for t in (high, middle, low))


def feature_kernel(group, parts, x_ref, f_ref, t_hbm, gram_ref, cross_ref, own_ref, xs, t_ref, rhs, acc, *rest):
    phis, (send, recv, local) = rest[:parts], rest[parts:]
    me = lax.axis_index("rhs")
    own, panel = x_ref.shape[1], t_ref.shape[1]
    chunk = own // parts
    load = pltpu.make_async_copy(t_hbm, t_ref, local)
    load.start()
    barrier = pltpu.get_barrier_semaphore()
    for d in range(1, group):
        pl.semaphore_signal(
            barrier, inc=1, device_id={"rhs": lax.rem(me + d, group)}, device_id_type=MESH
        )
    pl.semaphore_wait(barrier, group - 1)

    def sending(d):
        return pltpu.make_async_remote_copy(
            src_ref=x_ref,
            dst_ref=xs.at[d],
            send_sem=send.at[d],
            recv_sem=recv.at[d],
            device_id={"rhs": lax.rem(me + d, group)},
            device_id_type=MESH,
        )

    for d in range(1, group):
        sending(d).start()
    xs[0] = x_ref[...]
    acc[...] = jnp.zeros_like(acc)
    load.wait()
    scale = math.sqrt(2.0 * math.sqrt(2.0))

    @pl.loop(0, group)
    def _(d):
        @pl.when(d > 0)
        def _():
            sending(d).wait()

        block = lax.rem(me - d + group, group)
        for part in range(parts):
            x = xs[d, :, part * chunk : (part + 1) * chunk]
            high = x.astype(jnp.bfloat16)
            left = x - high.astype(jnp.float32)
            middle = left.astype(jnp.bfloat16)
            low = (left - middle.astype(jnp.float32)).astype(jnp.bfloat16)
            ones = jnp.ones(x.shape, jnp.bfloat16)
            rows = jnp.concatenate([high, high, middle, middle, high, low, ones], axis=0)
            turns = jnp.dot(f_ref[...], rows, preferred_element_type=jnp.float32)
            r = turns - jnp.round(turns)
            u = r * r
            s = jnp.full_like(u, SIN_TERMS[-1] * scale)
            for term in reversed(SIN_TERMS[:-1]):
                s = s * u + term * scale
            s = s * r
            phis[part][...] = (math.sqrt(2.0) - s * s).astype(jnp.bfloat16)
            mine = phis[part][pl.ds(pl.multiple_of(me * panel, panel), panel), :]
            rhs[part, :, :panel] = mine.T
            here = pl.multiple_of(block * own + part * chunk, chunk)
            rhs[part, :, panel:] = t_ref[pl.ds(here, chunk), :]
            acc[...] += jnp.dot(phis[part][...], rhs[part], preferred_element_type=jnp.float32)

        @pl.when(d == 0)
        def _():
            for part in range(parts):
                own_ref[part] = phis[part][...]

    gram_ref[...] = acc[:, :panel]
    cross_ref[...] = acc[:, panel:]


def panels(x, freqs, targets):
    group = lax.axis_size("rhs")
    depth, own = x.shape
    features = freqs.shape[0]
    panel = targets.shape[1]
    chunk = min(own, 512)
    parts = own // chunk
    sems = pltpu.SemaphoreType.DMA
    return pl.pallas_call(
        functools.partial(feature_kernel, group, parts),
        in_specs=[VMEM, VMEM, pl.BlockSpec(memory_space=pl.ANY)],
        out_specs=[VMEM] * 3,
        out_shape=[
            jax.ShapeDtypeStruct((features, panel), jnp.float32),
            jax.ShapeDtypeStruct((features, panel), jnp.float32),
            jax.ShapeDtypeStruct((parts, features, chunk), jnp.bfloat16),
        ],
        scratch_shapes=[
            pltpu.VMEM((group, depth, own), jnp.float32),
            pltpu.VMEM(targets.shape, targets.dtype),
            pltpu.VMEM((parts, chunk, 2 * panel), jnp.bfloat16),
            pltpu.VMEM((features, 2 * panel), jnp.float32),
        ]
        + [pltpu.VMEM((features, chunk), jnp.bfloat16)] * parts
        + [sems((group,)), sems((group,)), sems(())],
        compiler_params=pltpu.CompilerParams(collective_id=0, has_side_effects=True),
    )(x, freqs, targets)


def exchange(R, Z, w_ref, got, out, sems):
    send, recv, zsend, zrecv, psend, precv, csend, crecv = sems
    r, z = lax.axis_index("rows"), lax.axis_index("rhs")
    core, spot, half = lax.rem(r, 2), r // 2, R // 2

    def copy(src, dst, out_sem, in_sem, d, peer):
        return pltpu.make_async_remote_copy(
            src_ref=src,
            dst_ref=dst,
            send_sem=out_sem.at[d],
            recv_sem=in_sem.at[d],
            device_id=peer,
            device_id_type=MESH,
        )

    def scatter(d):
        peer = lax.rem(r + d, R)
        return copy(w_ref.at[peer], got.at[d], send, recv, d, {"rows": peer})

    def along(d):
        mine = out.at[r, z]
        return copy(mine, mine, zsend, zrecv, d, {"rhs": lax.rem(z + d, Z)})

    def across(d):
        peer = lax.rem(spot + d, half) * 2 + core
        return copy(out.at[r], out.at[r], psend, precv, d, {"rows": peer})

    def aside(d):
        where = out.at[lax.rem(spot - d + half, half) * 2 + core]
        return copy(where, where, csend, crecv, d, {"rows": r + 1 - 2 * core})

    def first():
        for d in range(1, R):
            scatter(d).start()

    def second():
        total = w_ref[r]
        for d in range(1, R):
            scatter(d).wait()
            total = total + got[d]
        out[r, z] = total
        for d in range(1, Z):
            along(d).start()

    def third():
        for d in range(1, Z):
            along(d).wait()
        for d in range(1, half):
            across(d).start()
        aside(0).start()

    def fourth():
        for d in range(1, half):
            across(d).wait()
            aside(d).start()

    def last():
        for d in range(half):
            aside(d).wait()

    return first, second, third, fourth, last


def invert_two(a, b, d):
    scale = 1.0 / (a * d - b * b)
    return d * scale, -b * scale, a * scale


def invert_four(p):
    e0, e1, e2 = invert_two(p[0][0], p[0][1], p[1][1])
    y00 = e0 * p[0][2] + e1 * p[1][2]
    y01 = e0 * p[0][3] + e1 * p[1][3]
    y10 = e1 * p[0][2] + e2 * p[1][2]
    y11 = e1 * p[0][3] + e2 * p[1][3]
    s0 = p[2][2] - (p[0][2] * y00 + p[1][2] * y10)
    s1 = p[2][3] - (p[0][2] * y01 + p[1][2] * y11)
    s2 = p[3][3] - (p[0][3] * y01 + p[1][3] * y11)
    t0, t1, t2 = invert_two(s0, s1, s2)
    q02 = -(y00 * t0 + y01 * t1)
    q03 = -(y00 * t1 + y01 * t2)
    q12 = -(y10 * t0 + y11 * t1)
    q13 = -(y10 * t1 + y11 * t2)
    q00 = e0 - (q02 * y00 + q03 * y01)
    q01 = e1 - (q02 * y10 + q03 * y11)
    q11 = e2 - (q12 * y10 + q13 * y11)
    return [
        [q00, q01, q02, q03],
        [q01, q11, q12, q13],
        [q02, q12, t0, t1],
        [q03, q13, t1, t2],
    ]


def invert_block(ref, dst):
    q = 4
    groups = TILE // 8
    a = [ref[8 * i : 8 * i + 8, :] for i in range(groups)]
    lane = lax.broadcasted_iota(jnp.int32, (8, TILE), 1)
    sub = lax.broadcasted_iota(jnp.int32, (8, TILE), 0)
    lane1 = lane[:1]
    for k in range(0, TILE, q):
        g, o = k // 8, k % 8
        c = [
            [jnp.broadcast_to(v[:, k + j : k + j + 1], (8, TILE)) for j in range(q)]
            for v in a
        ]
        if k == 0:
            p = [[c[g][j][o + i : o + i + 1, :] for j in range(q)] for i in range(q)]
        inv = invert_four(p)
        n = k + q
        if n < TILE:
            after = [jnp.broadcast_to(a[g][:, n + j : n + j + 1], (8, TILE)) for j in range(q)]
            mine = [[v[o + i : o + i + 1, :] for v in after] for i in range(q)]
            if n // 8 != g:
                after = [
                    jnp.broadcast_to(a[n // 8][:, n + j : n + j + 1], (8, TILE)) for j in range(q)
                ]
            below = [[v[n % 8 + i : n % 8 + i + 1, :] for v in after] for i in range(q)]
            t = [[sum(inv[i][b] * mine[b][j] for b in range(q)) for j in range(q)] for i in range(q)]
            p = [
                [
                    below[i][j] - sum(mine[b][i] * t[b][j] for b in range(q)) if j >= i else None
                    for j in range(q)
                ]
                for i in range(q)
            ]
        inside = jnp.logical_and(lane >= k, lane < k + q)
        pivot = [
            jnp.where(lane1 == k + i, 1.0, jnp.where(inside[:1], 0.0, a[g][o + i : o + i + 1, :]))
            for i in range(q)
        ]
        w = [sum(inv[i][j] * pivot[j] for j in range(q)) for i in range(q)]
        wb = [jnp.broadcast_to(v, (8, TILE)) for v in w]
        new = []
        for i in range(groups):
            v = jnp.where(inside, 0.0, a[i])
            v = v - ((c[i][0] * wb[0] + c[i][1] * wb[1]) + (c[i][2] * wb[2] + c[i][3] * wb[3]))
            if i == g:
                for j in range(q):
                    v = jnp.where(sub == o + j, wb[j], v)
            new.append(v)
        a = new
    for i in range(groups):
        dst[8 * i : 8 * i + 8, :] = a[i]


def solve_kernel(R, Z, count, w_ref, v_ref, coef_ref, low_ref, gram, right, lower, inverse, got, out, vgot, vout, *sems):
    rows, panel = w_ref.shape[1:]
    size = gram.shape[0]
    r, z = lax.axis_index("rows"), lax.axis_index("rhs")
    barrier = pltpu.get_barrier_semaphore()
    for d in range(1, R):
        pl.semaphore_signal(
            barrier, inc=1, device_id={"rows": lax.rem(r + d, R)}, device_id_type=MESH
        )
    for d in range(1, Z):
        pl.semaphore_signal(
            barrier, inc=1, device_id={"rhs": lax.rem(z + d, Z)}, device_id_type=MESH
        )
    pl.semaphore_wait(barrier, R + Z - 2)
    for stage in exchange(R, Z, w_ref, got, out, sems[:8]):
        stage()
    stages = exchange(R, Z, v_ref, vgot, vout, sems[8:])
    stages[0]()

    def spread(source, dest):
        for i in range(R):
            for j in range(Z):
                dest[i * rows : (i + 1) * rows, j * panel : (j + 1) * panel] = source[
                    i, j
                ] * (1.0 / count)

    spread(out, gram)
    row = lax.broadcasted_iota(jnp.int32, (TILE, TILE), 0)
    col = lax.broadcasted_iota(jnp.int32, (TILE, TILE), 1)
    eye = jnp.where(row == col, jnp.float32(ridge), 0.0)
    blocks = size // TILE
    dot = functools.partial(jnp.dot, precision=HIGHEST, preferred_element_type=jnp.float32)

    def at(i):
        return slice(i * TILE, (i + 1) * TILE)

    for k in range(blocks):
        gram[at(k), at(k)] += eye

    @pl.loop(0, blocks)
    def _(k):
        mine = pl.ds(pl.multiple_of(k * TILE, TILE), TILE)
        inverse[blocks] = gram[mine, mine]
        invert_block(inverse.at[blocks], inverse.at[k])
        gram_row = dot(inverse[k], gram[mine, :])

        @pl.loop(k + 1, blocks)
        def _(i):
            below = pl.ds(pl.multiple_of(i * TILE, TILE), TILE)
            left = gram[below, mine]
            lower[below, mine] = left
            gram[below, :] -= dot(left, gram_row)

        gram[mine, :] = gram_row
        for i, stage in enumerate(stages[1:]):
            pl.when(k == min(i, blocks - 1))(stage)

    spread(vout, right)
    for k in range(blocks):
        value = dot(inverse[k], right[at(k), :])
        right[at(k), :] = value
        if k + 1 < blocks:
            tail = slice((k + 1) * TILE, size)
            right[tail, :] -= dot(lower[tail, at(k)], value)
    for k in reversed(range(blocks)):
        value = right[at(k), :]
        coef_ref[at(k), :] = value
        low_ref[at(k), :] = value.astype(jnp.bfloat16)
        if k:
            right[: k * TILE, :] -= dot(gram[: k * TILE, at(k)], value)


def solve(count, w, v):
    R, Z = lax.axis_size("rows"), lax.axis_size("rhs")
    size, panel = w.shape
    rows, columns = size // R, Z * panel
    split = (R, rows, panel)
    sems = pltpu.SemaphoreType.DMA
    blocks = size // TILE
    big = pltpu.VMEM((R, Z, rows, panel), jnp.float32)
    return pl.pallas_call(
        functools.partial(solve_kernel, R, Z, count),
        out_shape=[
            jax.ShapeDtypeStruct((size, columns), jnp.float32),
            jax.ShapeDtypeStruct((size, columns), jnp.bfloat16),
        ],
        in_specs=[VMEM, VMEM],
        out_specs=[VMEM, VMEM],
        scratch_shapes=[
            pltpu.VMEM((size, size), jnp.float32),
            pltpu.VMEM((size, columns), jnp.float32),
            pltpu.VMEM((size, size), jnp.float32),
            pltpu.VMEM((blocks + 1, TILE, TILE), jnp.float32),
            pltpu.VMEM(split, jnp.float32),
            big,
            pltpu.VMEM(split, jnp.float32),
            big,
        ]
        + ([sems((R,))] * 2 + [sems((Z,))] * 2 + [sems((R,))] * 4) * 2,
        compiler_params=pltpu.CompilerParams(collective_id=1, has_side_effects=True),
    )(w.reshape(split), v.reshape(split))


def body(samples, freq_table, feature_seeds, phases, treatment_features):
    count = samples.shape[0] * lax.axis_size("rows") * lax.axis_size("rhs")
    turn = jnp.float32(1.0 / (2.0 * math.pi))
    high, middle, low = split_low(freq_table[feature_seeds] * turn)
    shift = jnp.stack(split_low(phases * turn), axis=1)
    shift = jnp.pad(shift, ((0, 0), (0, high.shape[1] - shift.shape[1])))
    freqs = jnp.concatenate([high, middle, high, middle, low, high, shift], axis=1)
    w, v, own = panels(samples.T, freqs, treatment_features)
    coefficients, low_coef = solve(count, w, v)
    fitted = lax.dot_general(
        own, low_coef, (((1,), (0,)), ((), ())), preferred_element_type=jnp.float32
    ).reshape(samples.shape[0], low_coef.shape[1])
    return (coefficients, fitted)


def solution(mesh):
    placed = (P(("rows", "rhs"), None), P(), P(), P(), P("rows", "rhs"))
    return jax.shard_map(
        body, mesh=mesh, in_specs=placed, out_specs=(P(), P(("rows", "rhs"), None)), check_vma=False
    )
```

```python
import functools
import math

import jax
import jax.numpy as jnp
from jax import lax
from jax.experimental import pallas as pl
from jax.experimental.pallas import tpu as pltpu
from jax.sharding import PartitionSpec as P

ridge = 0.05
MESH = pl.DeviceIdType.MESH
HIGHEST = lax.Precision.HIGHEST
VMEM = pl.BlockSpec(memory_space=pltpu.VMEM)
NT = (((1,), (1,)), ((), ()))
TILE = 128
SIN_TERMS = [3.1415926532437486, -5.167712741221454, 2.5501627947182053, -0.5992474048759052, 0.08203123002136099, -0.00700050017770637]


def split_low(x):
    high = lax.reduce_precision(x, 8, 7)
    rest = x - high
    middle = lax.reduce_precision(rest, 8, 7)
    low = rest - middle
    return tuple(t.astype(jnp.bfloat16) for t in (high, middle, low))


def feature_kernel(group, parts, x_ref, f_ref, t_hbm, gram_ref, cross_ref, own_ref, xs, t_ref, rhs, acc, *rest):
    phis, (send, recv, local) = rest[:parts], rest[parts:]
    me = lax.axis_index("rhs")
    own, panel = x_ref.shape[1], t_ref.shape[1]
    chunk = own // parts
    load = pltpu.make_async_copy(t_hbm, t_ref, local)
    load.start()
    barrier = pltpu.get_barrier_semaphore()
    for d in range(1, group):
        pl.semaphore_signal(
            barrier, inc=1, device_id={"rhs": lax.rem(me + d, group)}, device_id_type=MESH
        )
    pl.semaphore_wait(barrier, group - 1)

    def moving(d, way):
        block = me - way * (d - 1)
        return pltpu.make_async_remote_copy(
            src_ref=x_ref if isinstance(d, int) and d == 1 else xs.at[block],
            dst_ref=xs.at[block],
            send_sem=send.at[(way + 1) // 2, d],
            recv_sem=recv.at[(way + 1) // 2, d],
            device_id={"rhs": me + way},
            device_id_type=MESH,
        )

    def arriving(d, way):
        block = me - way * d
        return pltpu.make_async_remote_copy(
            src_ref=xs.at[block],
            dst_ref=xs.at[block],
            send_sem=send.at[(way + 1) // 2, d],
            recv_sem=recv.at[(way + 1) // 2, d],
            device_id={"rhs": me - way},
            device_id_type=MESH,
        )

    def inside(v):
        return jnp.logical_and(v >= 0, v < group)

    def pass_on(d, way):
        pl.when(jnp.logical_and(inside(me + way), inside(me - way * (d - 1))))(
            lambda: moving(d, way).start()
        )

    xs[me] = x_ref[...]
    for way in (1, -1):
        pass_on(1, way)
    acc[...] = jnp.zeros_like(acc)
    load.wait()
    near = jnp.minimum(me, group - 1 - me)
    scale = math.sqrt(2.0 * math.sqrt(2.0))

    @pl.loop(0, group)
    def _(d):
        for way in (1, -1):

            @pl.when(jnp.logical_and(d > 0, inside(me - way * d)))
            def _():
                arriving(d, way).wait_recv()

            pl.when(jnp.logical_and(d > 0, d + 1 < group))(lambda: pass_on(d + 1, way))

        step = (d + 1) // 2
        both = jnp.where(d % 2 == 1, me - step, me + step)
        single = jnp.where(me < group - 1 - me, me + d - near, me - d + near)
        block = jnp.where(d <= 2 * near, both, single)
        for part in range(parts):
            x = xs[block, :, part * chunk : (part + 1) * chunk]
            high = x.astype(jnp.bfloat16)
            left = x - high.astype(jnp.float32)
            middle = left.astype(jnp.bfloat16)
            low = (left - middle.astype(jnp.float32)).astype(jnp.bfloat16)
            ones = jnp.ones(x.shape, jnp.bfloat16)
            rows = jnp.concatenate([high, high, middle, middle, high, low, ones], axis=0)
            turns = jnp.dot(f_ref[...], rows, preferred_element_type=jnp.float32)
            r = turns - jnp.round(turns)
            u = r * r
            s = jnp.full_like(u, SIN_TERMS[-1] * scale)
            for term in reversed(SIN_TERMS[:-1]):
                s = s * u + term * scale
            s = s * r
            phis[part][...] = (math.sqrt(2.0) - s * s).astype(jnp.bfloat16)
            mine = phis[part][pl.ds(pl.multiple_of(me * panel, panel), panel), :]
            rhs[part, :, :panel] = mine.T
            here = pl.multiple_of(block * own + part * chunk, chunk)
            rhs[part, :, panel:] = t_ref[pl.ds(here, chunk), :]
            acc[...] += jnp.dot(phis[part][...], rhs[part], preferred_element_type=jnp.float32)

        @pl.when(d == 0)
        def _():
            for part in range(parts):
                own_ref[part] = phis[part][...]

    for d in range(1, group):
        for way in (1, -1):
            pl.when(jnp.logical_and(inside(me + way), inside(me - way * (d - 1))))(
                lambda: moving(d, way).wait_send()
            )
    gram_ref[...] = acc[:, :panel]
    cross_ref[...] = acc[:, panel:]


def panels(x, freqs, targets):
    group = lax.axis_size("rhs")
    depth, own = x.shape
    features = freqs.shape[0]
    panel = targets.shape[1]
    chunk = min(own, 512)
    parts = own // chunk
    sems = pltpu.SemaphoreType.DMA
    return pl.pallas_call(
        functools.partial(feature_kernel, group, parts),
        in_specs=[VMEM, VMEM, pl.BlockSpec(memory_space=pl.ANY)],
        out_specs=[VMEM] * 3,
        out_shape=[
            jax.ShapeDtypeStruct((features, panel), jnp.float32),
            jax.ShapeDtypeStruct((features, panel), jnp.float32),
            jax.ShapeDtypeStruct((parts, features, chunk), jnp.bfloat16),
        ],
        scratch_shapes=[
            pltpu.VMEM((group, depth, own), jnp.float32),
            pltpu.VMEM(targets.shape, targets.dtype),
            pltpu.VMEM((parts, chunk, 2 * panel), jnp.bfloat16),
            pltpu.VMEM((features, 2 * panel), jnp.float32),
        ]
        + [pltpu.VMEM((features, chunk), jnp.bfloat16)] * parts
        + [sems((2, group)), sems((2, group)), sems(())],
        compiler_params=pltpu.CompilerParams(collective_id=0, has_side_effects=True),
    )(x, freqs, targets)


def exchange(R, Z, w_ref, got, out, sems):
    send, recv, zsend, zrecv, psend, precv, csend, crecv = sems
    r, z = lax.axis_index("rows"), lax.axis_index("rhs")
    core, spot, half = lax.rem(r, 2), r // 2, R // 2

    def copy(src, dst, out_sem, in_sem, d, peer):
        return pltpu.make_async_remote_copy(
            src_ref=src,
            dst_ref=dst,
            send_sem=out_sem.at[d],
            recv_sem=in_sem.at[d],
            device_id=peer,
            device_id_type=MESH,
        )

    def scatter(d):
        peer = lax.rem(r + d, R)
        return copy(w_ref.at[peer], got.at[d], send, recv, d, {"rows": peer})

    def along(d):
        mine = out.at[r, z]
        return copy(mine, mine, zsend, zrecv, d, {"rhs": lax.rem(z + d, Z)})

    def across(d):
        peer = lax.rem(spot + d, half) * 2 + core
        return copy(out.at[r], out.at[r], psend, precv, d, {"rows": peer})

    def aside(d):
        where = out.at[lax.rem(spot - d + half, half) * 2 + core]
        return copy(where, where, csend, crecv, d, {"rows": r + 1 - 2 * core})

    def first():
        for d in range(1, R):
            scatter(d).start()

    def second():
        total = w_ref[r]
        for d in range(1, R):
            scatter(d).wait()
            total = total + got[d]
        out[r, z] = total
        for d in range(1, Z):
            along(d).start()

    def third():
        for d in range(1, Z):
            along(d).wait()
        for d in range(1, half):
            across(d).start()
        aside(0).start()

    def fourth():
        for d in range(1, half):
            across(d).wait()
            aside(d).start()

    def last():
        for d in range(half):
            aside(d).wait()

    return first, second, third, fourth, last


def invert_two(a, b, d):
    scale = 1.0 / (a * d - b * b)
    return d * scale, -b * scale, a * scale


def invert_four(p):
    e0, e1, e2 = invert_two(p[0][0], p[0][1], p[1][1])
    y00 = e0 * p[0][2] + e1 * p[1][2]
    y01 = e0 * p[0][3] + e1 * p[1][3]
    y10 = e1 * p[0][2] + e2 * p[1][2]
    y11 = e1 * p[0][3] + e2 * p[1][3]
    s0 = p[2][2] - (p[0][2] * y00 + p[1][2] * y10)
    s1 = p[2][3] - (p[0][2] * y01 + p[1][2] * y11)
    s2 = p[3][3] - (p[0][3] * y01 + p[1][3] * y11)
    t0, t1, t2 = invert_two(s0, s1, s2)
    q02 = -(y00 * t0 + y01 * t1)
    q03 = -(y00 * t1 + y01 * t2)
    q12 = -(y10 * t0 + y11 * t1)
    q13 = -(y10 * t1 + y11 * t2)
    q00 = e0 - (q02 * y00 + q03 * y01)
    q01 = e1 - (q02 * y10 + q03 * y11)
    q11 = e2 - (q12 * y10 + q13 * y11)
    return [
        [q00, q01, q02, q03],
        [q01, q11, q12, q13],
        [q02, q12, t0, t1],
        [q03, q13, t1, t2],
    ]


def invert_block(ref, dst):
    q = 4
    groups = TILE // 8
    a = [ref[8 * i : 8 * i + 8, :] for i in range(groups)]
    lane = lax.broadcasted_iota(jnp.int32, (8, TILE), 1)
    sub = lax.broadcasted_iota(jnp.int32, (8, TILE), 0)
    lane1 = lane[:1]
    for k in range(0, TILE, q):
        g, o = k // 8, k % 8
        c = [
            [jnp.broadcast_to(v[:, k + j : k + j + 1], (8, TILE)) for j in range(q)]
            for v in a
        ]
        if k == 0:
            p = [[c[g][j][o + i : o + i + 1, :] for j in range(q)] for i in range(q)]
        inv = invert_four(p)
        n = k + q
        if n < TILE:
            after = [jnp.broadcast_to(a[g][:, n + j : n + j + 1], (8, TILE)) for j in range(q)]
            mine = [[v[o + i : o + i + 1, :] for v in after] for i in range(q)]
            if n // 8 != g:
                after = [
                    jnp.broadcast_to(a[n // 8][:, n + j : n + j + 1], (8, TILE)) for j in range(q)
                ]
            below = [[v[n % 8 + i : n % 8 + i + 1, :] for v in after] for i in range(q)]
            t = [[sum(inv[i][b] * mine[b][j] for b in range(q)) for j in range(q)] for i in range(q)]
            p = [
                [
                    below[i][j] - sum(mine[b][i] * t[b][j] for b in range(q)) if j >= i else None
                    for j in range(q)
                ]
                for i in range(q)
            ]
        inside = jnp.logical_and(lane >= k, lane < k + q)
        pivot = [
            jnp.where(lane1 == k + i, 1.0, jnp.where(inside[:1], 0.0, a[g][o + i : o + i + 1, :]))
            for i in range(q)
        ]
        w = [sum(inv[i][j] * pivot[j] for j in range(q)) for i in range(q)]
        wb = [jnp.broadcast_to(v, (8, TILE)) for v in w]
        new = []
        for i in range(groups):
            v = jnp.where(inside, 0.0, a[i])
            v = v - ((c[i][0] * wb[0] + c[i][1] * wb[1]) + (c[i][2] * wb[2] + c[i][3] * wb[3]))
            if i == g:
                for j in range(q):
                    v = jnp.where(sub == o + j, wb[j], v)
            new.append(v)
        a = new
    for i in range(groups):
        dst[8 * i : 8 * i + 8, :] = a[i]


def solve_kernel(R, Z, count, w_ref, v_ref, coef_ref, low_ref, gram, right, lower, inverse, got, out, vgot, vout, *sems):
    rows, panel = w_ref.shape[1:]
    size = gram.shape[0]
    r, z = lax.axis_index("rows"), lax.axis_index("rhs")
    barrier = pltpu.get_barrier_semaphore()
    for d in range(1, R):
        pl.semaphore_signal(
            barrier, inc=1, device_id={"rows": lax.rem(r + d, R)}, device_id_type=MESH
        )
    for d in range(1, Z):
        pl.semaphore_signal(
            barrier, inc=1, device_id={"rhs": lax.rem(z + d, Z)}, device_id_type=MESH
        )
    pl.semaphore_wait(barrier, R + Z - 2)
    for stage in exchange(R, Z, w_ref, got, out, sems[:8]):
        stage()
    stages = exchange(R, Z, v_ref, vgot, vout, sems[8:])
    stages[0]()

    def spread(source, dest):
        for i in range(R):
            for j in range(Z):
                dest[i * rows : (i + 1) * rows, j * panel : (j + 1) * panel] = source[
                    i, j
                ] * (1.0 / count)

    spread(out, gram)
    row = lax.broadcasted_iota(jnp.int32, (TILE, TILE), 0)
    col = lax.broadcasted_iota(jnp.int32, (TILE, TILE), 1)
    eye = jnp.where(row == col, jnp.float32(ridge), 0.0)
    blocks = size // TILE
    dot = functools.partial(jnp.dot, precision=HIGHEST, preferred_element_type=jnp.float32)

    def at(i):
        return slice(i * TILE, (i + 1) * TILE)

    for k in range(blocks):
        gram[at(k), at(k)] += eye

    @pl.loop(0, blocks)
    def _(k):
        mine = pl.ds(pl.multiple_of(k * TILE, TILE), TILE)
        inverse[blocks] = gram[mine, mine]
        invert_block(inverse.at[blocks], inverse.at[k])
        gram_row = dot(inverse[k], gram[mine, :])

        @pl.loop(k + 1, blocks)
        def _(i):
            below = pl.ds(pl.multiple_of(i * TILE, TILE), TILE)
            left = gram[below, mine]
            lower[below, mine] = left
            gram[below, :] -= dot(left, gram_row)

        gram[mine, :] = gram_row
        for i, stage in enumerate(stages[1:]):
            pl.when(k == min(i, blocks - 1))(stage)

    spread(vout, right)
    for k in range(blocks):
        value = dot(inverse[k], right[at(k), :])
        right[at(k), :] = value
        if k + 1 < blocks:
            tail = slice((k + 1) * TILE, size)
            right[tail, :] -= dot(lower[tail, at(k)], value)
    for k in reversed(range(blocks)):
        value = right[at(k), :]
        coef_ref[at(k), :] = value
        low_ref[at(k), :] = value.astype(jnp.bfloat16)
        if k:
            right[: k * TILE, :] -= dot(gram[: k * TILE, at(k)], value)


def solve(count, w, v):
    R, Z = lax.axis_size("rows"), lax.axis_size("rhs")
    size, panel = w.shape
    rows, columns = size // R, Z * panel
    split = (R, rows, panel)
    sems = pltpu.SemaphoreType.DMA
    blocks = size // TILE
    big = pltpu.VMEM((R, Z, rows, panel), jnp.float32)
    return pl.pallas_call(
        functools.partial(solve_kernel, R, Z, count),
        out_shape=[
            jax.ShapeDtypeStruct((size, columns), jnp.float32),
            jax.ShapeDtypeStruct((size, columns), jnp.bfloat16),
        ],
        in_specs=[VMEM, VMEM],
        out_specs=[VMEM, VMEM],
        scratch_shapes=[
            pltpu.VMEM((size, size), jnp.float32),
            pltpu.VMEM((size, columns), jnp.float32),
            pltpu.VMEM((size, size), jnp.float32),
            pltpu.VMEM((blocks + 1, TILE, TILE), jnp.float32),
            pltpu.VMEM(split, jnp.float32),
            big,
            pltpu.VMEM(split, jnp.float32),
            big,
        ]
        + ([sems((R,))] * 2 + [sems((Z,))] * 2 + [sems((R,))] * 4) * 2,
        compiler_params=pltpu.CompilerParams(collective_id=1, has_side_effects=True),
    )(w.reshape(split), v.reshape(split))


def body(samples, freq_table, feature_seeds, phases, treatment_features):
    count = samples.shape[0] * lax.axis_size("rows") * lax.axis_size("rhs")
    turn = jnp.float32(1.0 / (2.0 * math.pi))
    high, middle, low = split_low(freq_table[feature_seeds] * turn)
    shift = jnp.stack(split_low(phases * turn), axis=1)
    shift = jnp.pad(shift, ((0, 0), (0, high.shape[1] - shift.shape[1])))
    freqs = jnp.concatenate([high, middle, high, middle, low, high, shift], axis=1)
    w, v, own = panels(samples.T, freqs, treatment_features)
    coefficients, low_coef = solve(count, w, v)
    fitted = lax.dot_general(
        own, low_coef, (((1,), (0,)), ((), ())), preferred_element_type=jnp.float32
    ).reshape(samples.shape[0], low_coef.shape[1])
    return (coefficients, fitted)


def solution(mesh):
    placed = (P(("rows", "rhs"), None), P(), P(), P(), P("rows", "rhs"))
    return jax.shard_map(
        body, mesh=mesh, in_specs=placed, out_specs=(P(), P(("rows", "rhs"), None)), check_vma=False
    )
```
